32 devices in a mesh: dom: 2 (over y), feat: 4 (over z), dp: 4 (over x, core).
Axes of the slice: x: 2, y: 2, z: 4, core: 2. Of those that a mesh axis runs over, the one named last changes fastest.
Arguments:
- layer_in: bfloat16 [32768, 2048], P(('dom', 'dp', 'feat')), parts along dimension 0, may hold values from -6 to 6
- grad_out: bfloat16 [32768, 2048], P(('dom', 'dp', 'feat')), parts along dimension 0, may hold values from -6 to 6
- in_proj: bfloat16 [2048, 256], replicated, may hold values from -0.125 to 0.125
- out_proj: bfloat16 [2048, 256], replicated, may hold values from -0.125 to 0.125
- queries: bfloat16 [2048, 65536], P(('dom', 'dp'), 'feat'), parts along dimension 0, may hold values from -0.00390625 to 0.00390625
- seq_ids: int32 [32, 1024], P(('dom', 'dp', 'feat')), parts along dimension 0, may hold values from 0 to 15, never falling along the last dimension, each value on 1 to 128 neighbouring positions
- valid_counts: int32 [512], P(('dom', 'dp', 'feat')), parts along dimension 0, may hold values from 16 to 128
- owner_order: int32 [2048], P(('dom', 'dp')), parts along dimension 0, may hold values from 0 to 1023, as said below
Outputs:
- scores: float32 [2048, 256], P(('dom', 'dp', 'feat')), parts along dimension 0
The draws below stay inside these ranges and needn't reach their ends.
There are 2 independent parts, one for each index of `dom`. The reference program is written for one: setup_inputs(seed, part) draws one part's arguments, and reference() takes and returns one part's arrays. A program takes and returns all parts, laid end to end along the dimension named above; an argument that names none is the same for every part. Nothing has to cross between parts.
Inputs may be any that keep to these rules, and one draw needn't show every extreme that they name: `seq_ids`: each row numbers the 16 sequences of one block in order, never falling; every number appears. `owner_order`: within each aligned block of 256 rows, a permutation of that block's row numbers.
All inputs are finite; a program needn't handle non-finite values.
Results may differ from the reference program's by a relative error of at most 0.005.
Values may be sent and summed in bfloat16 or wider, within the bound.
A program may use at most 64 MiB of HBM per device.

```python
import math
import jax
import jax.numpy as jnp
import numpy as np
from jax import lax

D = 2048
R = 256
FEATS = 65536
SEQ_DEV = 16
SEQ_LEN = 64
WIN = 128
TOK_DEV = 1024
GROUPS = 16
TOKENS = 16384
SEQUENCES = 256
Q_DP = 256
QUERIES = 1024


def draw_owner_order(key, part):
    blocks = QUERIES // Q_DP
    subkeys = jax.random.split(jax.random.fold_in(key, 17), blocks)

    def one_order(subkey):
        return jax.random.permutation(subkey, Q_DP).astype(jnp.int32)
    orders = jax.vmap(one_order)(subkeys)
    offsets = (jnp.arange(blocks, dtype=jnp.int32) * Q_DP)[:, None]
    return (orders + offsets).reshape(QUERIES).astype(jnp.int32)


def plant(drawn, rng, least, top_value):
    place = [jax.random.randint(jax.random.fold_in(rng, axis), (), 0, length) for axis, length in enumerate(drawn.shape)]
    longest = drawn.shape.index(max(drawn.shape))
    neighbour = place[:longest] + [(place[longest] + 1) % drawn.shape[longest]] + place[longest + 1:]
    return drawn.at[tuple(place)].set(least).at[tuple(neighbour)].set(top_value)


def strengthened(entries, own_key, source, target, shards_of, factor):
    owner, partner = [(jnp.arange(entries.shape[axis_at]) // (entries.shape[axis_at] // shards_of)).reshape([-1 if axis == axis_at else 1 for axis in range(entries.ndim)]) for axis_at in (source, target)]
    chosen = jax.random.permutation(own_key, shards_of)[partner]
    strong = (owner == chosen) | (owner == (partner + shards_of // 2) % shards_of)
    return jnp.where(strong, factor * entries, entries)


def block_levels(key, extent, pieces, least, largest):
    def one(dim, shards_of):
        heights = jax.random.uniform(jax.random.fold_in(jax.random.fold_in(key, 6), dim), (shards_of,), jnp.float32, least / len(pieces), largest / len(pieces))
        return jnp.repeat(jnp.exp(heights), extent[dim] // shards_of).reshape((-1,) + (1,) * (len(extent) - dim - 1))

    level = one(*pieces[0])
    for cut in pieces[1:]:
        level = level * one(*cut)
    return level


def split_up(count, total, bound, lean):
    loads = [(1 << 20) // math.isqrt(standing ** lean) + 1 for standing in range(2, count + 1)]
    spare, given = total - bound - (count - 1), [1] * (count - 1)
    while spare > 0:
        free = [i for i in range(count - 1) if given[i] < bound]
        mass, left = sum([loads[i] for i in free]), spare
        for i in free:
            more = min(bound - given[i], max(1, left * loads[i] // mass), spare)
            given[i] = given[i] + more
            spare = spare - more
    return np.array([bound] + given)


def uneven(rng, count, total, reach, skew):
    if count == 2:
        one = jax.random.randint(rng, (), max(1, total - reach), min(reach, total - 1) + 1)
        return jnp.stack([one, total - one])
    lengths = jnp.asarray(split_up(count, total, reach, skew), jnp.int32)
    couples = (count - 1) // 2
    source_of, receiver = lengths[1:1 + 2 * couples:2], lengths[2:2 + 2 * couples:2]
    slack = jnp.minimum(source_of - 1, reach - receiver)
    passed = jax.random.randint(jax.random.fold_in(rng, 1), (couples,), 0, 1 << 20) % (slack + 1)
    lengths = lengths.at[1:1 + 2 * couples:2].set(source_of - passed).at[2:2 + 2 * couples:2].set(receiver + passed)
    return lengths[jax.random.permutation(jax.random.fold_in(rng, 2), count)]


def scatter_about(key, extent, width, limit, cuts=(), kind=jnp.bfloat16):
    values = width * jax.random.normal(key, extent, jnp.float32)
    if cuts:
        values = values * block_levels(key, extent, cuts, -0.22, 0.18)
    return jnp.clip(values, -limit, limit).astype(kind)


def bell_draw_with(key, dims, deviation, reach, pieces, heavy, held_as=jnp.bfloat16):
    entries = deviation * jax.random.normal(key, dims, jnp.float32)
    if pieces:
        entries = entries * block_levels(key, dims, pieces, -0.22, 0.18)
    return jnp.clip(strengthened(entries, jax.random.fold_in(key, 3), *heavy), -reach, reach).astype(held_as)


def setup_inputs(seed: int = 0, part: int = 0) -> dict:
    splits = jax.random.split(jax.random.key(seed), 9)
    own_keys = jax.random.split(jax.random.fold_in(splits[8], part), 9)
    return {
        "layer_in": scatter_about(own_keys[0], (TOKENS, D), 1.0, 6.0, ((0, 16),)),
        "grad_out": scatter_about(own_keys[1], (TOKENS, D), 1.0, 6.0, ((0, 16),)),
        "in_proj": scatter_about(splits[2], (D, R), D ** -0.5, 0.125),
        "out_proj": scatter_about(splits[3], (D, R), D ** -0.5, 0.125),
        "queries": bell_draw_with(own_keys[4], (QUERIES, FEATS), (FEATS * SEQ_LEN) ** -0.5, 0.00390625, ((0, 4), (1, 4)), (1, 0, 4, 2.0)),
        "seq_ids": jax.vmap(lambda own: jnp.searchsorted(jnp.cumsum(uneven(own, SEQ_DEV, TOK_DEV, WIN, 0)), jnp.arange(TOK_DEV), side="right"))(jax.random.split(own_keys[5], GROUPS)).reshape((GROUPS, TOK_DEV)).astype(jnp.int32),
        "valid_counts": plant(jax.random.randint(own_keys[6], (SEQUENCES,), WIN // 8, WIN + 1), jax.random.fold_in(own_keys[6], 1), WIN // 8, WIN).astype(jnp.int32),
        "owner_order": draw_owner_order(jax.random.fold_in(jax.random.fold_in(splits[8], part), 71), part),
    }


def sequence_grads(in_low, out_low, labels, counts):
    member = (labels[:, None] == jnp.arange(SEQ_DEV, dtype=jnp.int32)[None, :]).astype(jnp.int32)
    seg_len = jnp.sum(member, axis=0).astype(jnp.int32)
    starts = (jnp.cumsum(seg_len) - seg_len).astype(jnp.int32)
    position = jnp.arange(TOK_DEV, dtype=jnp.int32) - starts[labels]
    counted = (position < counts[labels]).astype(jnp.float32)
    weighted = in_low.astype(jnp.float32) * counted[:, None]
    member_f = member.astype(jnp.float32)
    grads = jnp.einsum("ts,ti,tj->sij", member_f, weighted, out_low.astype(jnp.float32), precision=lax.Precision.HIGHEST)
    return grads.reshape(SEQ_DEV, R * R).astype(jnp.bfloat16)


def reference(layer_in, grad_out, in_proj, out_proj, queries, seq_ids, valid_counts, owner_order):
    layer_blocks = layer_in.reshape(GROUPS, TOK_DEV, D)
    grad_blocks = grad_out.reshape(GROUPS, TOK_DEV, D)
    count_blocks = valid_counts.reshape(GROUPS, SEQ_DEV)

    def one_block(inputs):
        layer_rows, grad_rows, labels, counts = inputs
        in_low = jnp.dot(layer_rows, in_proj, preferred_element_type=jnp.float32).astype(jnp.bfloat16)
        out_low = jnp.dot(grad_rows, out_proj, preferred_element_type=jnp.float32).astype(jnp.bfloat16)
        return sequence_grads(in_low, out_low, labels, counts)

    seq_grads = lax.map(one_block, (layer_blocks, grad_blocks, seq_ids, count_blocks))
    seq_grads = seq_grads.reshape(SEQUENCES, R * R)
    score = lax.dot_general(queries, seq_grads, (((1,), (1,)), ((), ())), preferred_element_type=jnp.float32)
    return jnp.take(score, owner_order, axis=0)
```

```python
import functools

import jax
import jax.numpy as jnp
from jax import lax
from jax.experimental import pallas as pl
from jax.experimental.pallas import tpu as pltpu
from jax.sharding import PartitionSpec as P

MESH = pl.DeviceIdType.MESH
F32 = jnp.float32
BF16 = jnp.bfloat16


def grads_kernel(steps, tile, x_ref, g_ref, wi_ref, wo_ref, ids_ref, cnt_ref, out_ref, in_t, out_low):
    step = pl.program_id(0)
    at = pl.ds(pl.multiple_of(step * tile, tile), tile)
    low = jnp.dot(x_ref[...], wi_ref[...], preferred_element_type=F32)
    in_t[:, at] = low.astype(BF16).astype(F32).T
    out_low[at, :] = jnp.dot(g_ref[...], wo_ref[...], preferred_element_type=F32).astype(BF16)

    @pl.when(step == steps - 1)
    def _():
        width, seqs, _ = out_ref.shape
        tokens = in_t.shape[1]
        labels = ids_ref[...]
        rows = lax.broadcasted_iota(jnp.int32, (seqs, tokens), 0)
        cols = lax.broadcasted_iota(jnp.int32, (seqs, tokens), 1)
        starts = jnp.sum((labels < rows).astype(F32), axis=1, keepdims=True).astype(jnp.int32)
        mask = ((labels == rows) & (cols - starts < cnt_ref[...])).astype(F32)
        some = 16

        def body(k, carry):
            span = pl.ds(pl.multiple_of(k * some, some), some)
            left = in_t[span, :][:, None, :] * mask[None, :, :]
            left = left.reshape(some * seqs, tokens).astype(BF16)
            got = jnp.dot(left, out_low[...], preferred_element_type=F32)
            out_ref[span] = got.astype(BF16).reshape(some, seqs, width)
            return carry

        lax.fori_loop(0, width // some, body, 0)


def seq_grads_of(layer_in, grad_out, in_proj, out_proj, seq_ids, valid_counts):
    tokens, model = layer_in.shape
    width = in_proj.shape[1]
    seqs = valid_counts.shape[0]
    tile = min(256, tokens)
    steps = tokens // tile
    return pl.pallas_call(
        functools.partial(grads_kernel, steps, tile),
        grid=(steps,),
        out_shape=jax.ShapeDtypeStruct((width, seqs, width), BF16),
        in_specs=[
            pl.BlockSpec((tile, model), lambda i: (i, 0)),
            pl.BlockSpec((tile, model), lambda i: (i, 0)),
            pl.BlockSpec((model, width), lambda i: (0, 0)),
            pl.BlockSpec((model, width), lambda i: (0, 0)),
            pl.BlockSpec((1, tokens), lambda i: (0, 0)),
            pl.BlockSpec((seqs, 1), lambda i: (0, 0)),
        ],
        out_specs=pl.BlockSpec((width, seqs, width), lambda i: (0, 0, 0)),
        scratch_shapes=[pltpu.VMEM((width, tokens), F32), pltpu.VMEM((tokens, width), BF16)],
        compiler_params=pltpu.CompilerParams(vmem_limit_bytes=48 * 1024 * 1024),
    )(layer_in, grad_out, in_proj, out_proj, seq_ids, valid_counts.reshape(seqs, 1))


def flip(i, m):
    bit = 1
    while bit <= m:
        if m & bit:
            i = i + bit - 2 * bit * (lax.div(i, bit) % 2)
        bit *= 2
    return i


def score_kernel(fn, dn, chunks, grads, queries, order, out, held, q_buf, acc, perm, piece, landed,
                 q_sem, own_sem, a_send, a_recv, d_send, d_recv, r_send, r_recv):
    me_f = lax.axis_index("feat")
    me_d = lax.axis_index("dp")
    slab = held.shape[2]
    seqs = held.shape[3]
    width = held.shape[4]
    q_rows = queries.shape[0]
    rows = q_rows // fn
    part = slab // chunks
    bits = []
    bit = dn // 2
    while bit >= 1:
        bits.append(bit)
        bit //= 2

    barrier = pltpu.get_barrier_semaphore()
    for r in range(1, fn):
        pl.semaphore_signal(barrier, inc=1, device_id={"feat": flip(me_f, r)}, device_id_type=MESH)
    for b in bits:
        pl.semaphore_signal(barrier, inc=1, device_id={"dp": flip(me_d, b)}, device_id_type=MESH)
    pl.semaphore_wait(barrier, fn - 1 + len(bits))

    def across(r, c):
        other = flip(me_f, r)
        return pltpu.make_async_remote_copy(
            src_ref=grads.at[pl.ds(other * slab + c * part, part)],
            dst_ref=held.at[me_f, me_d, pl.ds(c * part, part)],
            send_sem=a_send.at[r, c],
            recv_sem=a_recv.at[r, c],
            device_id={"feat": other},
            device_id_type=MESH,
        )

    def own(c):
        return pltpu.make_async_copy(
            grads.at[pl.ds(me_f * slab + c * part, part)],
            held.at[me_f, me_d, pl.ds(c * part, part)],
            own_sem.at[c],
        )

    def along(r, m, b, c):
        block = held.at[flip(me_f, r), flip(me_d, m), pl.ds(c * part, part)]
        return pltpu.make_async_remote_copy(
            src_ref=block,
            dst_ref=block,
            send_sem=d_send.at[r, m + b, c],
            recv_sem=d_recv.at[r, m + b, c],
            device_id={"dp": flip(me_d, b)},
            device_id_type=MESH,
        )

    q_copy = pltpu.make_async_copy(queries, q_buf, q_sem)
    for c in range(chunks):
        own(c).start()
    for r in range(1, fn):
        for c in range(chunks):
            across(r, c).start()
    q_copy.start()

    at_row = lax.broadcasted_iota(jnp.int32, (q_rows, q_rows), 0)
    perm[...] = ((order[...] % q_rows) == at_row).astype(F32).T

    def masks_before(k):
        got = [0]
        for b in bits[:k]:
            got = got + [m + b for m in got]
        return got

    def stage(k, r, c):
        if k == 0:
            if r == 0:
                own(c).wait()
            else:
                across(r, c).wait_recv()
        else:
            for m in masks_before(k - 1):
                along(r, m, bits[k - 1], c).wait_recv()
        if k < len(bits):
            for m in masks_before(k):
                along(r, m, bits[k], c).start()

    def score(r, c):
        source = flip(me_f, r)

        def body(i, total):
            left = q_buf[:, pl.ds(pl.multiple_of(i * width, width), width)]
            right = held[source, :, i].reshape(dn * seqs, width)
            return total + lax.dot_general(left, right, (((1,), (1,)), ((), ())), preferred_element_type=F32)

        start = jnp.zeros(acc.shape, F32) if c == 0 else acc[...]
        acc[...] = lax.fori_loop(c * part, (c + 1) * part, body, start)
        if c == chunks - 1:
            ordered = jnp.dot(perm[...], acc[...], precision=lax.Precision.HIGHEST, preferred_element_type=F32)
            piece[:, source] = ordered.reshape(fn, rows, dn * seqs)

            def send(t, carry):
                other = lax.rem(me_f + t, fn)
                pltpu.make_async_remote_copy(
                    src_ref=piece.at[other, source],
                    dst_ref=landed.at[me_f, source],
                    send_sem=r_send.at[other],
                    recv_sem=r_recv.at[me_f],
                    device_id={"feat": other},
                    device_id_type=MESH,
                ).start()
                return carry

            lax.fori_loop(1, fn, send, 0)

    events = [(r, c) for r in range(fn) for c in range(chunks)]
    last = len(bits)
    for e in range(len(events) + last):
        for k in range(last + 1):
            if 0 <= e - k < len(events):
                stage(k, *events[e - k])
        if e - last == 0:
            q_copy.wait()
        if e >= last:
            score(*events[e - last])

    total = piece[me_f]
    for r in range(1, fn):
        other = flip(me_f, r)
        pltpu.make_async_copy(landed.at[other], landed.at[other], r_recv.at[other]).wait()
        total = total + landed[other]
    out[...] = total
    for r in range(1, fn):
        other = flip(me_f, r)
        pltpu.make_async_copy(piece.at[other], piece.at[other], r_send.at[other]).wait()
        for c in range(chunks):
            across(r, c).wait_send()
    for r, c in events:
        for k, b in enumerate(bits):
            for m in masks_before(k):
                along(r, m, b, c).wait_send()


def scores_of(fn, dn, grads, queries, owner_order):
    width, seqs, _ = grads.shape
    q_rows, feats = queries.shape
    slab = width // fn
    rows = q_rows // fn
    chunks = max(1, min(4, slab // 16))
    dma = pltpu.SemaphoreType.DMA
    return pl.pallas_call(
        functools.partial(score_kernel, fn, dn, chunks),
        out_shape=jax.ShapeDtypeStruct((fn, rows, dn * seqs), F32),
        in_specs=[
            pl.BlockSpec(memory_space=pl.ANY),
            pl.BlockSpec(memory_space=pl.ANY),
            pl.BlockSpec(memory_space=pltpu.VMEM),
        ],
        out_specs=pl.BlockSpec(memory_space=pltpu.VMEM),
        scratch_shapes=[
            pltpu.VMEM((fn, dn, slab, seqs, width), BF16),
            pltpu.VMEM((q_rows, feats), BF16),
            pltpu.VMEM((q_rows, dn * seqs), F32),
            pltpu.VMEM((q_rows, q_rows), F32),
            pltpu.VMEM((fn, fn, rows, dn * seqs), F32),
            pltpu.VMEM((fn, fn, rows, dn * seqs), F32),
            dma,
            dma((chunks,)),
            dma((fn, chunks)),
            dma((fn, chunks)),
            dma((fn, dn, chunks)),
            dma((fn, dn, chunks)),
            dma((fn,)),
            dma((fn,)),
        ],
        compiler_params=pltpu.CompilerParams(
            collective_id=0, has_side_effects=True, vmem_limit_bytes=56 * 1024 * 1024
        ),
    )(grads, queries, owner_order.reshape(1, q_rows))


def local(fn, dn, layer_in, grad_out, in_proj, out_proj, queries, seq_ids, valid_counts, owner_order):
    grads = seq_grads_of(layer_in, grad_out, in_proj, out_proj, seq_ids, valid_counts)
    got = scores_of(fn, dn, grads, queries, owner_order)
    rows = got.shape[1]
    seqs = valid_counts.shape[0]
    return got.reshape(fn, rows, dn, seqs).transpose(1, 2, 0, 3).reshape(rows, dn * fn * seqs)


def solution(mesh):
    in_specs = (
        P(("dom", "dp", "feat"), None),
        P(("dom", "dp", "feat"), None),
        P(),
        P(),
        P(("dom", "dp"), "feat"),
        P(("dom", "dp", "feat"), None),
        P(("dom", "dp", "feat")),
        P(("dom", "dp")),
    )
    out_specs = P(("dom", "dp", "feat"), None)
    body = functools.partial(local, mesh.shape["feat"], mesh.shape["dp"])
    return jax.shard_map(body, mesh=mesh, in_specs=in_specs, out_specs=out_specs, check_vma=False)
```

```python
import functools

import jax
import jax.numpy as jnp
from jax import lax
from jax.experimental import pallas as pl
from jax.experimental.pallas import tpu as pltpu
from jax.sharding import PartitionSpec as P

MESH = pl.DeviceIdType.MESH
F32 = jnp.float32
BF16 = jnp.bfloat16


def grads_kernel(steps, tile, x_ref, g_ref, wi_ref, wo_ref, ids_ref, cnt_ref, out_ref, in_t, out_low):
    step = pl.program_id(0)
    at = pl.ds(pl.multiple_of(step * tile, tile), tile)
    low = jnp.dot(x_ref[...], wi_ref[...], preferred_element_type=F32)
    in_t[:, at] = low.astype(BF16).astype(F32).T
    out_low[at, :] = jnp.dot(g_ref[...], wo_ref[...], preferred_element_type=F32).astype(BF16)

    @pl.when(step == steps - 1)
    def _():
        width, seqs, _ = out_ref.shape
        tokens = in_t.shape[1]
        labels = ids_ref[...]
        rows = lax.broadcasted_iota(jnp.int32, (seqs, tokens), 0)
        cols = lax.broadcasted_iota(jnp.int32, (seqs, tokens), 1)
        starts = jnp.sum((labels < rows).astype(F32), axis=1, keepdims=True).astype(jnp.int32)
        one_r = lax.broadcasted_iota(jnp.int32, (seqs, seqs), 0)
        one_c = lax.broadcasted_iota(jnp.int32, (seqs, seqs), 1)
        counts = jnp.where(one_r == one_c, cnt_ref[...].astype(F32), 0.0)
        counts = jnp.sum(counts, axis=1, keepdims=True).astype(jnp.int32)
        mask = ((labels == rows) & (cols - starts < counts)).astype(F32)
        some = 16

        def body(k, carry):
            span = pl.ds(pl.multiple_of(k * some, some), some)
            left = in_t[span, :][:, None, :] * mask[None, :, :]
            left = left.reshape(some * seqs, tokens).astype(BF16)
            got = jnp.dot(left, out_low[...], preferred_element_type=F32)
            out_ref[span] = got.astype(BF16).reshape(some, seqs, width)
            return carry

        lax.fori_loop(0, width // some, body, 0)


def seq_grads_of(layer_in, grad_out, in_proj, out_proj, seq_ids, valid_counts):
    tokens, model = layer_in.shape
    width = in_proj.shape[1]
    seqs = valid_counts.shape[0]
    tile = min(256, tokens)
    steps = tokens // tile
    return pl.pallas_call(
        functools.partial(grads_kernel, steps, tile),
        grid=(steps,),
        out_shape=jax.ShapeDtypeStruct((width, seqs, width), BF16),
        in_specs=[
            pl.BlockSpec((tile, model), lambda i: (i, 0)),
            pl.BlockSpec((tile, model), lambda i: (i, 0)),
            pl.BlockSpec((model, width), lambda i: (0, 0)),
            pl.BlockSpec((model, width), lambda i: (0, 0)),
            pl.BlockSpec((1, tokens), lambda i: (0, 0)),
            pl.BlockSpec((1, seqs), lambda i: (0, 0)),
        ],
        out_specs=pl.BlockSpec((width, seqs, width), lambda i: (0, 0, 0)),
        scratch_shapes=[pltpu.VMEM((width, tokens), F32), pltpu.VMEM((tokens, width), BF16)],
        compiler_params=pltpu.CompilerParams(vmem_limit_bytes=67043328),
    )(layer_in, grad_out, in_proj, out_proj, seq_ids, valid_counts.reshape(1, seqs))


def flip(i, m):
    bit = 1
    while bit <= m:
        if m & bit:
            i = i + bit - 2 * bit * (lax.div(i, bit) % 2)
        bit *= 2
    return i


def score_kernel(fn, dn, chunks, grads, queries, order, out, held, q_buf, acc, perm, piece, landed,
                 q_sem, own_sem, a_send, a_recv, d_send, d_recv, r_send, r_recv):
    me_f = lax.axis_index("feat")
    me_d = lax.axis_index("dp")
    slab = held.shape[2]
    seqs = held.shape[3]
    width = held.shape[4]
    q_rows = queries.shape[0]
    rows = q_rows // fn
    part = slab // chunks
    bits = []
    bit = dn // 2
    while bit >= 1:
        bits.append(bit)
        bit //= 2

    barrier = pltpu.get_barrier_semaphore()
    for r in range(1, fn):
        pl.semaphore_signal(barrier, inc=1, device_id={"feat": flip(me_f, r)}, device_id_type=MESH)
    for b in bits:
        pl.semaphore_signal(barrier, inc=1, device_id={"dp": flip(me_d, b)}, device_id_type=MESH)
    pl.semaphore_wait(barrier, fn - 1 + len(bits))

    def across(r, c):
        other = flip(me_f, r)
        return pltpu.make_async_remote_copy(
            src_ref=grads.at[pl.ds(other * slab + c * part, part)],
            dst_ref=held.at[me_f, me_d, pl.ds(c * part, part)],
            send_sem=a_send.at[r, c],
            recv_sem=a_recv.at[r, c],
            device_id={"feat": other},
            device_id_type=MESH,
        )

    def own(c):
        return pltpu.make_async_copy(
            grads.at[pl.ds(me_f * slab + c * part, part)],
            held.at[me_f, me_d, pl.ds(c * part, part)],
            own_sem.at[c],
        )

    def along(r, m, b, c):
        block = held.at[flip(me_f, r), flip(me_d, m), pl.ds(c * part, part)]
        return pltpu.make_async_remote_copy(
            src_ref=block,
            dst_ref=block,
            send_sem=d_send.at[r, m + b, c],
            recv_sem=d_recv.at[r, m + b, c],
            device_id={"dp": flip(me_d, b)},
            device_id_type=MESH,
        )

    q_copy = pltpu.make_async_copy(queries, q_buf, q_sem)
    for c in range(chunks):
        own(c).start()
    for r in range(1, fn):
        for c in range(chunks):
            across(r, c).start()
    q_copy.start()

    at_row = lax.broadcasted_iota(jnp.int32, (q_rows, q_rows), 0)
    perm[...] = ((order[...] % q_rows) == at_row).astype(F32).T

    def masks_before(k):
        got = [0]
        for b in bits[:k]:
            got = got + [m + b for m in got]
        return got

    def stage(k, r, c):
        if k == 0:
            if r == 0:
                own(c).wait()
            else:
                across(r, c).wait_recv()
        else:
            for m in masks_before(k - 1):
                along(r, m, bits[k - 1], c).wait_recv()
        if k < len(bits):
            for m in masks_before(k):
                along(r, m, bits[k], c).start()

    def score(r, c):
        source = flip(me_f, r)

        blocks = [held[source, :, c * part + i].reshape(dn * seqs, width) for i in range(part)]
        span = slice(c * part * width, (c + 1) * part * width)
        got = lax.dot_general(
            q_buf[:, span], jnp.concatenate(blocks, axis=1), (((1,), (1,)), ((), ())), preferred_element_type=F32
        )
        acc[...] = got if c == 0 else acc[...] + got
        if c == chunks - 1:
            ordered = jnp.dot(perm[...], acc[...], precision=lax.Precision.HIGHEST, preferred_element_type=F32)
            piece[:, source] = ordered.reshape(fn, rows, dn * seqs)

            def send(t, carry):
                other = lax.rem(me_f + t, fn)
                pltpu.make_async_remote_copy(
                    src_ref=piece.at[other, source],
                    dst_ref=landed.at[me_f, source],
                    send_sem=r_send.at[other],
                    recv_sem=r_recv.at[me_f],
                    device_id={"feat": other},
                    device_id_type=MESH,
                ).start()
                return carry

            lax.fori_loop(1, fn, send, 0)

    events = [(r, c) for r in range(fn) for c in range(chunks)]
    last = len(bits)
    for e in range(len(events) + last):
        for k in range(last + 1):
            if 0 <= e - k < len(events):
                stage(k, *events[e - k])
        if e - last == 0:
            q_copy.wait()
        if e >= last:
            score(*events[e - last])

    total = piece[me_f]
    for r in range(1, fn):
        other = flip(me_f, r)
        pltpu.make_async_copy(landed.at[other], landed.at[other], r_recv.at[other]).wait()
        total = total + landed[other]
    out[...] = total
    for r in range(1, fn):
        other = flip(me_f, r)
        pltpu.make_async_copy(piece.at[other], piece.at[other], r_send.at[other]).wait()
        for c in range(chunks):
            across(r, c).wait_send()
    for r, c in events:
        for k, b in enumerate(bits):
            for m in masks_before(k):
                along(r, m, b, c).wait_send()


def scores_of(fn, dn, grads, queries, owner_order):
    width, seqs, _ = grads.shape
    q_rows, feats = queries.shape
    slab = width // fn
    rows = q_rows // fn
    chunks = max(1, min(4, slab // 16))
    dma = pltpu.SemaphoreType.DMA
    return pl.pallas_call(
        functools.partial(score_kernel, fn, dn, chunks),
        out_shape=jax.ShapeDtypeStruct((fn, rows, dn * seqs), F32),
        in_specs=[
            pl.BlockSpec(memory_space=pl.ANY),
            pl.BlockSpec(memory_space=pl.ANY),
            pl.BlockSpec(memory_space=pltpu.VMEM),
        ],
        out_specs=pl.BlockSpec(memory_space=pltpu.VMEM),
        scratch_shapes=[
            pltpu.VMEM((fn, dn, slab, seqs, width), BF16),
            pltpu.VMEM((q_rows, feats), BF16),
            pltpu.VMEM((q_rows, dn * seqs), F32),
            pltpu.VMEM((q_rows, q_rows), F32),
            pltpu.VMEM((fn, fn, rows, dn * seqs), F32),
            pltpu.VMEM((fn, fn, rows, dn * seqs), F32),
            dma,
            dma((chunks,)),
            dma((fn, chunks)),
            dma((fn, chunks)),
            dma((fn, dn, chunks)),
            dma((fn, dn, chunks)),
            dma((fn,)),
            dma((fn,)),
        ],
        compiler_params=pltpu.CompilerParams(
            collective_id=0, has_side_effects=True, vmem_limit_bytes=67043328
        ),
    )(grads, queries, owner_order.reshape(1, q_rows))


def local(fn, dn, layer_in, grad_out, in_proj, out_proj, queries, seq_ids, valid_counts, owner_order):
    grads = seq_grads_of(layer_in, grad_out, in_proj, out_proj, seq_ids, valid_counts)
    got = scores_of(fn, dn, grads, queries, owner_order)
    rows = got.shape[1]
    seqs = valid_counts.shape[0]
    return got.reshape(fn, rows, dn, seqs).transpose(1, 2, 0, 3).reshape(rows, dn * fn * seqs)


def solution(mesh):
    in_specs = (
        P(("dom", "dp", "feat"), None),
        P(("dom", "dp", "feat"), None),
        P(),
        P(),
        P(("dom", "dp"), "feat"),
        P(("dom", "dp", "feat"), None),
        P(("dom", "dp", "feat")),
        P(("dom", "dp")),
    )
    out_specs = P(("dom", "dp", "feat"), None)
    body = functools.partial(local, mesh.shape["feat"], mesh.shape["dp"])
    return jax.shard_map(body, mesh=mesh, in_specs=in_specs, out_specs=out_specs, check_vma=False)
```

```python
import functools

import jax
import jax.numpy as jnp
from jax import lax
from jax.experimental import pallas as pl
from jax.experimental.pallas import tpu as pltpu
from jax.sharding import PartitionSpec as P

MESH = pl.DeviceIdType.MESH
F32 = jnp.float32
BF16 = jnp.bfloat16


def grads_kernel(steps, tile, x_ref, g_ref, wi_ref, wo_ref, ids_ref, cnt_ref, out_ref, in_t, out_low):
    step = pl.program_id(0)
    at = pl.ds(pl.multiple_of(step * tile, tile), tile)
    low = jnp.dot(x_ref[...], wi_ref[...], preferred_element_type=F32)
    in_t[:, at] = low.astype(BF16).astype(F32).T
    out_low[at, :] = jnp.dot(g_ref[...], wo_ref[...], preferred_element_type=F32).astype(BF16)

    @pl.when(step == steps - 1)
    def _():
        width, seqs, _ = out_ref.shape
        tokens = in_t.shape[1]
        labels = ids_ref[...]
        rows = lax.broadcasted_iota(jnp.int32, (seqs, tokens), 0)
        cols = lax.broadcasted_iota(jnp.int32, (seqs, tokens), 1)
        starts = jnp.sum((labels < rows).astype(F32), axis=1, keepdims=True).astype(jnp.int32)
        one_r = lax.broadcasted_iota(jnp.int32, (seqs, seqs), 0)
        one_c = lax.broadcasted_iota(jnp.int32, (seqs, seqs), 1)
        counts = jnp.where(one_r == one_c, cnt_ref[...].astype(F32), 0.0)
        counts = jnp.sum(counts, axis=1, keepdims=True).astype(jnp.int32)
        mask = ((labels == rows) & (cols - starts < counts)).astype(F32)
        some = 16

        def body(k, carry):
            span = pl.ds(pl.multiple_of(k * some, some), some)
            left = in_t[span, :][:, None, :] * mask[None, :, :]
            left = left.reshape(some * seqs, tokens).astype(BF16)
            got = jnp.dot(left, out_low[...], preferred_element_type=F32)
            out_ref[span] = got.astype(BF16).reshape(some, seqs, width)
            return carry

        lax.fori_loop(0, width // some, body, 0, unroll=2)


def seq_grads_of(layer_in, grad_out, in_proj, out_proj, seq_ids, valid_counts):
    tokens, model = layer_in.shape
    width = in_proj.shape[1]
    seqs = valid_counts.shape[0]
    tile = min(256, tokens)
    steps = tokens // tile
    return pl.pallas_call(
        functools.partial(grads_kernel, steps, tile),
        grid=(steps,),
        out_shape=jax.ShapeDtypeStruct((width, seqs, width), BF16),
        in_specs=[
            pl.BlockSpec((tile, model), lambda i: (i, 0)),
            pl.BlockSpec((tile, model), lambda i: (i, 0)),
            pl.BlockSpec((model, width), lambda i: (0, 0)),
            pl.BlockSpec((model, width), lambda i: (0, 0)),
            pl.BlockSpec((1, tokens), lambda i: (0, 0)),
            pl.BlockSpec((1, seqs), lambda i: (0, 0)),
        ],
        out_specs=pl.BlockSpec((width, seqs, width), lambda i: (0, 0, 0)),
        scratch_shapes=[pltpu.VMEM((width, tokens), F32), pltpu.VMEM((tokens, width), BF16)],
        compiler_params=pltpu.CompilerParams(vmem_limit_bytes=67043328),
    )(layer_in, grad_out, in_proj, out_proj, seq_ids, valid_counts.reshape(1, seqs))


def flip(i, m):
    bit = 1
    while bit <= m:
        if m & bit:
            i = i + bit - 2 * bit * (lax.div(i, bit) % 2)
        bit *= 2
    return i


def score_kernel(fn, dn, chunks, grads, queries, order, out, held, q_buf, acc, perm, piece, landed,
                 q_sem, own_sem, a_send, a_recv, d_send, d_recv, r_send, r_recv):
    me_f = lax.axis_index("feat")
    me_d = lax.axis_index("dp")
    slab = held.shape[2]
    seqs = held.shape[3]
    width = held.shape[4]
    q_rows = queries.shape[0]
    rows = q_rows // fn
    part = slab // chunks
    bits = []
    bit = dn // 2
    while bit >= 1:
        bits.append(bit)
        bit //= 2

    barrier = pltpu.get_barrier_semaphore()
    for r in range(1, fn):
        pl.semaphore_signal(barrier, inc=1, device_id={"feat": flip(me_f, r)}, device_id_type=MESH)
    for b in bits:
        pl.semaphore_signal(barrier, inc=1, device_id={"dp": flip(me_d, b)}, device_id_type=MESH)
    pl.semaphore_wait(barrier, fn - 1 + len(bits))

    def across(r, c):
        other = flip(me_f, r)
        return pltpu.make_async_remote_copy(
            src_ref=grads.at[pl.ds(other * slab + c * part, part)],
            dst_ref=held.at[me_f, me_d, pl.ds(c * part, part)],
            send_sem=a_send.at[r, c],
            recv_sem=a_recv.at[r, c],
            device_id={"feat": other},
            device_id_type=MESH,
        )

    def own(c):
        return pltpu.make_async_copy(
            grads.at[pl.ds(me_f * slab + c * part, part)],
            held.at[me_f, me_d, pl.ds(c * part, part)],
            own_sem.at[c],
        )

    def along(r, m, b, c):
        block = held.at[flip(me_f, r), flip(me_d, m), pl.ds(c * part, part)]
        return pltpu.make_async_remote_copy(
            src_ref=block,
            dst_ref=block,
            send_sem=d_send.at[r, m + b, c],
            recv_sem=d_recv.at[r, m + b, c],
            device_id={"dp": flip(me_d, b)},
            device_id_type=MESH,
        )

    q_copy = pltpu.make_async_copy(queries, q_buf, q_sem)
    for c in range(chunks):
        own(c).start()
    for r in range(1, fn):
        for c in range(chunks):
            across(r, c).start()
    q_copy.start()

    at_row = lax.broadcasted_iota(jnp.int32, (q_rows, q_rows), 0)
    perm[...] = ((order[...] % q_rows) == at_row).astype(F32).T

    def masks_before(k):
        got = [0]
        for b in bits[:k]:
            got = got + [m + b for m in got]
        return got

    def stage(k, r, c):
        if k == 0:
            if r == 0:
                own(c).wait()
            else:
                across(r, c).wait_recv()
        else:
            for m in masks_before(k - 1):
                along(r, m, bits[k - 1], c).wait_recv()
        if k < len(bits):
            for m in masks_before(k):
                along(r, m, bits[k], c).start()

    def score(r, c):
        source = flip(me_f, r)

        blocks = [held[source, :, c * part + i].reshape(dn * seqs, width) for i in range(part)]
        span = slice(c * part * width, (c + 1) * part * width)
        got = lax.dot_general(
            q_buf[:, span], jnp.concatenate(blocks, axis=1), (((1,), (1,)), ((), ())), preferred_element_type=F32
        )
        acc[...] = got if c == 0 else acc[...] + got
        if c == chunks - 1:
            ordered = jnp.dot(perm[...], acc[...], precision=lax.Precision.HIGHEST, preferred_element_type=F32)
            piece[:, source] = ordered.reshape(fn, rows, dn * seqs)

            def send(t, carry):
                other = lax.rem(me_f + t, fn)
                pltpu.make_async_remote_copy(
                    src_ref=piece.at[other, source],
                    dst_ref=landed.at[me_f, source],
                    send_sem=r_send.at[other],
                    recv_sem=r_recv.at[me_f],
                    device_id={"feat": other},
                    device_id_type=MESH,
                ).start()
                return carry

            lax.fori_loop(1, fn, send, 0)

    events = [(r, c) for r in range(fn) for c in range(chunks)]
    last = len(bits)
    for e in range(len(events) + last):
        for k in range(last + 1):
            if 0 <= e - k < len(events):
                stage(k, *events[e - k])
        if e - last == 0:
            q_copy.wait()
        if e >= last:
            score(*events[e - last])

    total = piece[me_f]
    for r in range(1, fn):
        other = flip(me_f, r)
        pltpu.make_async_copy(landed.at[other], landed.at[other], r_recv.at[other]).wait()
        total = total + landed[other]
    out[...] = total
    for r in range(1, fn):
        other = flip(me_f, r)
        pltpu.make_async_copy(piece.at[other], piece.at[other], r_send.at[other]).wait()
        for c in range(chunks):
            across(r, c).wait_send()
    for r, c in events:
        for k, b in enumerate(bits):
            for m in masks_before(k):
                along(r, m, b, c).wait_send()


def scores_of(fn, dn, grads, queries, owner_order):
    width, seqs, _ = grads.shape
    q_rows, feats = queries.shape
    slab = width // fn
    rows = q_rows // fn
    chunks = max(1, min(8, slab // 8))
    dma = pltpu.SemaphoreType.DMA
    return pl.pallas_call(
        functools.partial(score_kernel, fn, dn, chunks),
        out_shape=jax.ShapeDtypeStruct((fn, rows, dn * seqs), F32),
        in_specs=[
            pl.BlockSpec(memory_space=pl.ANY),
            pl.BlockSpec(memory_space=pl.ANY),
            pl.BlockSpec(memory_space=pltpu.VMEM),
        ],
        out_specs=pl.BlockSpec(memory_space=pltpu.VMEM),
        scratch_shapes=[
            pltpu.VMEM((fn, dn, slab, seqs, width), BF16),
            pltpu.VMEM((q_rows, feats), BF16),
            pltpu.VMEM((q_rows, dn * seqs), F32),
            pltpu.VMEM((q_rows, q_rows), F32),
            pltpu.VMEM((fn, fn, rows, dn * seqs), F32),
            pltpu.VMEM((fn, fn, rows, dn * seqs), F32),
            dma,
            dma((chunks,)),
            dma((fn, chunks)),
            dma((fn, chunks)),
            dma((fn, dn, chunks)),
            dma((fn, dn, chunks)),
            dma((fn,)),
            dma((fn,)),
        ],
        compiler_params=pltpu.CompilerParams(
            collective_id=0, has_side_effects=True, vmem_limit_bytes=67043328
        ),
    )(grads, queries, owner_order.reshape(1, q_rows))


def local(fn, dn, layer_in, grad_out, in_proj, out_proj, queries, seq_ids, valid_counts, owner_order):
    grads = seq_grads_of(layer_in, grad_out, in_proj, out_proj, seq_ids, valid_counts)
    got = scores_of(fn, dn, grads, queries, owner_order)
    rows = got.shape[1]
    seqs = valid_counts.shape[0]
    return got.reshape(fn, rows, dn, seqs).transpose(1, 2, 0, 3).reshape(rows, dn * fn * seqs)


def solution(mesh):
    in_specs = (
        P(("dom", "dp", "feat"), None),
        P(("dom", "dp", "feat"), None),
        P(),
        P(),
        P(("dom", "dp"), "feat"),
        P(("dom", "dp", "feat"), None),
        P(("dom", "dp", "feat")),
        P(("dom", "dp")),
    )
    out_specs = P(("dom", "dp", "feat"), None)
    body = functools.partial(local, mesh.shape["feat"], mesh.shape["dp"])
    return jax.shard_map(body, mesh=mesh, in_specs=in_specs, out_specs=out_specs, check_vma=False)
```
